512 devices in a mesh: blk: 64 (over z_hi, y, core), rep: 8 (over z_lo, x).
Axes of the slice: x: 4, y: 8, z: 8 (z_hi: 4, z_lo: 2; z = z_hi * 2 + z_lo), core: 2. Of those that a mesh axis runs over, the one named last changes fastest.
Arguments:
- features: bfloat16 [32768, 128], P('blk'), may hold values from -6 to 6
- weight: bfloat16 [128, 256], replicated, may hold values from -0.5 to 0.5
- tile_vals: bfloat16 [64, 8, 8, 12, 128, 128], P('blk', 'rep'), may hold values from -0.0390625 to 0.0390625
- tile_pos: int32 [64, 8, 8, 12], P('blk', 'rep'), may hold values from 0 to 15, as said below
- tile_count: int32 [64, 8, 8], P('blk', 'rep'), may hold values from 1 to 12, as said below
- cotangent: bfloat16 [32768, 256], P(('blk', 'rep')), may hold values from -6 to 6
Outputs:
- activations: bfloat16 [32768, 256], P(('blk', 'rep'))
- feat_grad: bfloat16 [32768, 128], P(('blk', 'rep'))
- weight_grad: float32 [128, 256], replicated
The draws below stay inside these ranges and needn't reach their ends.
Inputs may be any that keep to these rules, and one draw needn't show every extreme that they name: `tile_pos`: within one row group, copy and section the entries are distinct. `tile_count`: row group 0 has all 12 slots live in every copy and section.
All inputs are finite; a program needn't handle non-finite values.
Results may differ from the reference program's by a relative error of at most 0.014.
Values may be sent and summed in bfloat16 or wider, within the bound.
A program may use at most 128 MiB of HBM per device.

```python
import jax
import jax.numpy as jnp
from jax import lax

FEAT = 128
HID = 256
TILE = 128
NB_DEV = 4
TILES = 12
SECTIONS = 8
NODES = 32768
N_BLK = 64
N_REP = 8


def draw_tile_pos(key, part):
    cells = NB_DEV * NB_DEV
    scores = jax.random.randint(key, (N_BLK, N_REP, SECTIONS, cells), 0, 1 << 20) * cells
    scores = scores + jnp.arange(cells, dtype=jnp.int32)
    ordering = jnp.argsort(scores, axis=-1, stable=True)
    return ordering[..., :TILES].astype(jnp.int32)


def draw_tile_count(key, part):
    base_count = jax.random.randint(jax.random.fold_in(key, 1), (N_BLK, N_REP, SECTIONS), 1, TILES // 2 + 1)
    group_extra = jax.random.randint(jax.random.fold_in(key, 2), (N_BLK, 1, 1), 0, TILES // 2 + 1)
    counted = jnp.minimum(base_count + group_extra, TILES)
    counted = counted.at[0].set(TILES)
    return counted.astype(jnp.int32)


def level_of(own_key, shape, shards, least, largest):
    loudness, own = 1.0, jax.random.fold_in(own_key, 6)
    for axis_at, shards_of in shards:
        heights = jnp.exp(jax.random.uniform(jax.random.fold_in(own, axis_at), (shards_of,), jnp.float32, least / len(shards), largest / len(shards)))
        loudness = loudness * jnp.repeat(heights, shape[axis_at] // shards_of).reshape([-1 if axis == axis_at else 1 for axis in range(len(shape))])
    return loudness


def normal_values(key, extent, spread, bound, pieces=(), kind=jnp.bfloat16):
    result = jax.random.normal(key, extent, jnp.float32) * spread
    if len(pieces) > 0:
        result = level_of(key, extent, pieces, -0.22, 0.18) * result
    return jnp.clip(result, min=-bound, max=bound).astype(kind)


def setup_inputs(seed: int = 0) -> dict:
    streams_of = jax.random.split(jax.random.key(seed), 7)
    return {
        "features": normal_values(streams_of[0], (NODES, FEAT), 1.0, 6.0, ((0, 64),)),
        "weight": normal_values(streams_of[1], (FEAT, HID), FEAT ** -0.5, 0.5),
        "tile_vals": normal_values(streams_of[2], (N_BLK, N_REP, SECTIONS, TILES, TILE, TILE), (N_BLK * TILES * TILE // NB_DEV) ** -0.5, 0.0390625, ((0, 64), (1, 8))),
        "tile_pos": draw_tile_pos(jax.random.fold_in(streams_of[6], 71), 0),
        "tile_count": draw_tile_count(jax.random.fold_in(streams_of[6], 71), 0),
        "cotangent": normal_values(streams_of[5], (NODES, HID), 1.0, 6.0, ((0, 512),)),
    }


def gelu_tanh(value):
    return jax.nn.gelu(value, approximate=True)

def reference(features, weight, tile_vals, tile_pos, tile_count, cotangent):
    section_count = N_BLK // N_REP
    hidden = jnp.dot(features, weight, preferred_element_type=jnp.float32).astype(jnp.bfloat16)
    hidden_blocks = hidden.reshape(N_BLK * NB_DEV, TILE, HID)
    rep_ids = jnp.arange(N_REP, dtype=jnp.int32)[:, None]
    section_ids = jnp.arange(section_count, dtype=jnp.int32)[None, :]
    offsets = rep_ids + section_ids * N_REP
    live_mask = (jnp.arange(TILES, dtype=jnp.int32)[None, None, None, :] < tile_count[..., None]).astype(jnp.float32)
    block_ids = jnp.arange(NB_DEV, dtype=jnp.int32)

    def forward_group(group):
        columns = (group - offsets) % N_BLK
        positions = tile_pos[group]
        col_index = columns[..., None] * NB_DEV + positions % NB_DEV
        picked = hidden_blocks[col_index].astype(jnp.float32)
        tile_block = tile_vals[group].astype(jnp.float32) * live_mask[group][..., None, None]
        product = jnp.einsum('rstik,rstkf->rstif', tile_block, picked)
        placing = ((positions // NB_DEV)[..., None] == block_ids).astype(jnp.float32)
        return jnp.einsum('rstn,rstif->nif', placing, product).reshape(NB_DEV * TILE, HID)
    pre = lax.map(forward_group, jnp.arange(N_BLK, dtype=jnp.int32)).reshape(NODES, HID)
    outputs, pullback = jax.vjp(gelu_tanh, pre)
    activations = outputs.astype(jnp.bfloat16)
    pre_grad = pullback(cotangent.astype(jnp.float32))[0].astype(jnp.bfloat16)
    grad_blocks = pre_grad.reshape(N_BLK * NB_DEV, TILE, HID)
    rep_grid = jnp.broadcast_to(rep_ids, (N_REP, section_count))
    section_grid = jnp.broadcast_to(section_ids, (N_REP, section_count))

    def backward_group(column):
        sources = (column + offsets) % N_BLK
        positions = tile_pos[sources, rep_grid, section_grid]
        tile_block = tile_vals[sources, rep_grid, section_grid].astype(jnp.float32)
        tile_block = tile_block * live_mask[sources, rep_grid, section_grid][..., None, None]
        row_index = sources[..., None] * NB_DEV + positions // NB_DEV
        picked = grad_blocks[row_index].astype(jnp.float32)
        product = jnp.einsum('rstki,rstkf->rstif', tile_block, picked)
        placing = ((positions % NB_DEV)[..., None] == block_ids).astype(jnp.float32)
        return jnp.einsum('rstn,rstif->nif', placing, product).reshape(NB_DEV * TILE, HID)
    hidden_grad = lax.map(backward_group, jnp.arange(N_BLK, dtype=jnp.int32)).reshape(NODES, HID)
    hidden_grad = hidden_grad.astype(jnp.bfloat16)
    weight_grad = jnp.dot(features.T, hidden_grad, preferred_element_type=jnp.float32)
    feat_grad = jnp.dot(hidden_grad, weight.T, preferred_element_type=jnp.float32).astype(jnp.bfloat16)
    return (activations, feat_grad, weight_grad)
```

```python
import jax
import jax.numpy as jnp
from jax import lax
from jax.sharding import PartitionSpec as P


def gelu_tanh(value):
    return jax.nn.gelu(value, approximate=True)


def skewed(block, sign):
    blks, reps = lax.axis_size("blk"), lax.axis_size("rep")
    route = [
        (b * reps + r, ((b + sign * r) % blks) * reps + r) for b in range(blks) for r in range(reps)
    ]
    return lax.ppermute(block, ("blk", "rep"), route)


def split_dot(left, right):
    high = left.astype(jnp.bfloat16)
    low = (left - high.astype(jnp.float32)).astype(jnp.bfloat16)
    return jnp.dot(high, right, preferred_element_type=jnp.float32) + jnp.dot(
        low, right, preferred_element_type=jnp.float32
    )


def dense_adjacency(tiles, positions, counts, group, blocks):
    sections, slots = positions.shape
    cells = jnp.arange(blocks * blocks, dtype=jnp.int32)
    live = jnp.arange(slots, dtype=jnp.int32)[None, :] < counts[:, None]
    hits = (positions[:, None, :] == cells[None, :, None]) & live[:, None, :]
    slot_of = jnp.argmax(hits, axis=-1).astype(jnp.int32)
    filled = jnp.any(hits, axis=-1)
    order = (group - jnp.arange(sections, dtype=jnp.int32)) % sections
    slot_of, filled = slot_of[order], filled[order]
    picked = tiles[order[:, None], slot_of]
    return jnp.where(filled[..., None, None], picked, jnp.zeros((), tiles.dtype)).reshape(
        sections, blocks, blocks, tiles.shape[-2], tiles.shape[-1]
    )


def local(features, weight, tile_vals, tile_pos, tile_count, cotangent):
    rep_size = lax.axis_size("rep")
    blk_size = lax.axis_size("blk")
    blk_index = lax.axis_index("blk")
    tile_size = tile_vals.shape[-1]
    rows, feat = features.shape
    blocks = rows // tile_size
    rings = [[r + k * rep_size for k in range(blk_size // rep_size)] for r in range(rep_size)]

    adjacency = dense_adjacency(
        tile_vals[0, 0], tile_pos[0, 0], tile_count[0, 0], blk_index // rep_size, blocks
    )
    gathered = lax.all_gather(skewed(features, 1), "blk", axis_index_groups=rings)
    columns = gathered.reshape(-1, blocks, tile_size, feat)
    mixed = jnp.einsum(
        "jnmik,jmkf->nif", adjacency, columns, preferred_element_type=jnp.float32
    ).reshape(rows, feat)
    mixed = lax.psum_scatter(mixed, "rep", scatter_dimension=0, tiled=True)

    pre = split_dot(mixed, weight)
    outputs, pullback = jax.vjp(gelu_tanh, pre)
    activations = outputs.astype(jnp.bfloat16)
    pre_grad = pullback(cotangent.astype(jnp.float32))[0].astype(jnp.bfloat16)
    weight_grad = lax.dot_general(
        mixed.astype(jnp.bfloat16),
        pre_grad,
        (((0,), (0,)), ((), ())),
        preferred_element_type=jnp.float32,
    )
    weight_grad = lax.psum(lax.psum(weight_grad, "rep"), "blk")
    row_grad = lax.dot_general(
        pre_grad, weight, (((1,), (1,)), ((), ())), preferred_element_type=jnp.float32
    ).astype(jnp.bfloat16)
    row_grad = lax.all_gather(row_grad, "rep", axis=0, tiled=True).reshape(blocks, tile_size, feat)
    partial = jnp.einsum(
        "jnmik,nif->jmkf", adjacency, row_grad, preferred_element_type=jnp.float32
    ).reshape(-1, rows, feat)
    partial = lax.psum_scatter(partial, "blk", scatter_dimension=0, axis_index_groups=rings)
    partial = skewed(partial, -1)
    feat_grad = lax.psum_scatter(partial, "rep", scatter_dimension=0, tiled=True)
    return (activations, feat_grad.astype(jnp.bfloat16), weight_grad)


def solution(mesh):
    placed = (
        P("blk", None),
        P(),
        P("blk", "rep", None, None, None, None),
        P("blk", "rep", None, None),
        P("blk", "rep", None),
        P(("blk", "rep"), None),
    )
    return jax.shard_map(
        local,
        mesh=mesh,
        in_specs=placed,
        out_specs=(P(("blk", "rep"), None), P(("blk", "rep"), None), P()),
        check_vma=False,
    )
```

```python
import functools
import math

import jax
import jax.numpy as jnp
from jax import lax
from jax.experimental import pallas as pl
from jax.experimental.pallas import tpu as pltpu
from jax.sharding import PartitionSpec as P

MESH = pl.DeviceIdType.MESH


def place_kernel(blocks, pos_ref, count_ref, tiles_ref, out_ref):
    section = pl.program_id(0)
    tile = tiles_ref.shape[-1]
    out_ref[...] = jnp.zeros_like(out_ref)
    for slot in range(tiles_ref.shape[1]):

        @pl.when(slot < count_ref[section])
        def _():
            position = pos_ref[section, slot]
            row = pl.multiple_of(lax.div(position, blocks) * tile, tile)
            column = pl.multiple_of(lax.rem(position, blocks) * tile, tile)
            out_ref[0, pl.ds(row, tile), pl.ds(column, tile)] = tiles_ref[0, slot]


def dense_adjacency(tiles, positions, counts, blocks):
    sections, slots, tile, _ = tiles.shape
    side = blocks * tile
    return pl.pallas_call(
        functools.partial(place_kernel, blocks),
        grid_spec=pltpu.PrefetchScalarGridSpec(
            num_scalar_prefetch=2,
            grid=(sections,),
            in_specs=[pl.BlockSpec((1, slots, tile, tile), lambda j, p, c: (j, 0, 0, 0))],
            out_specs=pl.BlockSpec((1, side, side), lambda j, p, c: (j, 0, 0)),
        ),
        out_shape=jax.ShapeDtypeStruct((sections, side, side), tiles.dtype),
    )(positions, counts, tiles)


def gelu_and_slope(value):
    scale = math.sqrt(2.0 / math.pi)
    square = value * value
    bend = jnp.tanh(scale * (value + 0.044715 * (square * value)))
    half = 0.5 * (1.0 + bend)
    slope = half + 0.5 * value * (1.0 - bend * bend) * (
        scale * (1.0 + 3.0 * 0.044715 * square)
    )
    return value * half, slope


def dot(left, right, contract=(1, 0)):
    return lax.dot_general(
        left,
        right,
        (((contract[0],), (contract[1],)), ((), ())),
        preferred_element_type=jnp.float32,
    )


def layer_kernel(
    blks,
    reps,
    features_ref,
    weight_ref,
    adj_ref,
    cot_ref,
    act_ref,
    feat_ref,
    wgrad_ref,
    xs,
    total,
    ysend,
    yrecv,
    urows,
    psend,
    precv,
    hsend,
    hrecv,
    wsend,
    wrecv,
    ring_out,
    ring_in,
    low_out,
    low_in,
    wall,
    x_ss,
    x_rs,
    y_ss,
    y_rs,
    u_ss,
    u_rs,
    p_ss,
    p_rs,
    h_ss,
    h_rs,
    w_ss,
    w_rs,
    ring_ss,
    ring_rs,
    low_ss,
    low_rs,
    g_ss,
    g_rs,
):
    b = lax.axis_index("blk")
    r = lax.axis_index("rep")
    sections = blks // reps
    share = cot_ref.shape[0]
    rows = features_ref.shape[0]
    wshare = wsend.shape[1]

    def ahead(j):
        return (lax.rem(b + r + reps * j, blks), r)

    def behind(j):
        return (lax.rem(b - r - reps * j + 2 * blks, blks), r)

    def rep_peer(i):
        return (b, lax.rem(r + i, reps))

    def ring_peer(i):
        return (lax.rem(b + reps * i, blks), r)

    def low_peer(i):
        low = lax.rem(b, reps)
        return (b - low + lax.rem(low + i, reps), r)

    def remote(src, dst, ss, rs, device):
        return pltpu.make_async_remote_copy(
            src_ref=src,
            dst_ref=dst,
            send_sem=ss,
            recv_sem=rs,
            device_id=device,
            device_id_type=MESH,
        )

    barrier = pltpu.get_barrier_semaphore()

    def greet(device):
        pl.semaphore_signal(barrier, inc=1, device_id=device, device_id_type=MESH)

    @pl.when(r != 0)
    def _():
        greet(ahead(0))
        greet(behind(0))

    for j in range(1, sections):
        greet(ahead(j))
        greet(behind(j))
        greet(ring_peer(j))
    for i in range(1, reps):
        greet(rep_peer(i))
        greet(low_peer(i))
    greeted = 3 * (sections - 1) + 2 * (reps - 1)
    pl.semaphore_wait(barrier, jnp.where(r == 0, greeted, greeted + 2))

    def x_copy(j):
        return remote(features_ref, xs.at[j], x_ss.at[j], x_rs.at[j], ahead(j))

    own_x = pltpu.make_async_copy(features_ref, xs.at[0], x_rs.at[0])

    @pl.when(r != 0)
    def _():
        x_copy(0).start()

    @pl.when(r == 0)
    def _():
        own_x.start()

    for j in range(1, sections):
        x_copy(j).start()

    @pl.when(r != 0)
    def _():
        x_copy(0).wait_recv()

    @pl.when(r == 0)
    def _():
        own_x.wait()

    total[...] = dot(adj_ref[0], xs[0])

    def forward(j, carry):
        x_copy(j).wait_recv()
        total[...] += dot(adj_ref[j], xs[j])
        return carry

    lax.fori_loop(1, sections, forward, 0)

    ysend[...] = total[...].reshape(reps, share, total.shape[1])

    def to_peers(copy, count):
        for i in range(1, count):
            copy(i).start()

    def take(copy, count):
        for i in range(1, count):
            copy(i).wait_recv()

    def y_copy(i):
        peer = rep_peer(i)
        return remote(ysend.at[peer[1]], yrecv.at[i], y_ss.at[i], y_rs.at[i], peer)

    to_peers(y_copy, reps)
    mixed = ysend[r]
    for i in range(1, reps):
        y_copy(i).wait_recv()
        mixed = mixed + yrecv[i]

    weight = weight_ref[...]
    high = mixed.astype(jnp.bfloat16)
    low = (mixed - high.astype(jnp.float32)).astype(jnp.bfloat16)
    act, slope = gelu_and_slope(dot(high, weight) + dot(low, weight))
    act_ref[...] = act.astype(jnp.bfloat16)
    pre_grad = (cot_ref[...].astype(jnp.float32) * slope).astype(jnp.bfloat16)
    urows[r] = dot(pre_grad, weight, (1, 1)).astype(jnp.bfloat16)

    def u_copy(i):
        return remote(urows.at[r], urows.at[r], u_ss.at[i], u_rs.at[i], rep_peer(i))

    def u_arrival(i):
        source = lax.rem(r - i + reps, reps)
        return remote(urows.at[source], urows.at[source], u_ss.at[i], u_rs.at[i], rep_peer(i))

    to_peers(u_copy, reps)
    wsend[...] = dot(high, pre_grad, (0, 0)).reshape(wsend.shape)

    def w_copy(i):
        peer = rep_peer(i)
        return remote(wsend.at[peer[1]], wrecv.at[i], w_ss.at[i], w_rs.at[i], peer)

    to_peers(w_copy, reps)
    take(u_arrival, reps)
    flipped = urows[...].reshape(rows, urows.shape[2]).T

    def p_copy(j):
        return remote(psend.at[j], precv.at[j], p_ss.at[j], p_rs.at[j], behind(j))

    own_p = pltpu.make_async_copy(psend.at[0], precv.at[0], p_rs.at[0])
    psend[0] = dot(flipped, adj_ref[0]).astype(jnp.bfloat16)

    @pl.when(r != 0)
    def _():
        p_copy(0).start()

    @pl.when(r == 0)
    def _():
        own_p.start()

    def backward(j, carry):
        psend[j] = dot(flipped, adj_ref[j]).astype(jnp.bfloat16)
        p_copy(j).start()
        return carry

    lax.fori_loop(1, sections, backward, 0)

    part = wsend[r]
    for i in range(1, reps):
        w_copy(i).wait_recv()
        part = part + wrecv[i]
    ring_out[...] = part

    def ring_copy(i):
        return remote(ring_out, ring_in.at[i], ring_ss.at[i], ring_rs.at[i], ring_peer(i))

    to_peers(ring_copy, sections)
    for i in range(1, sections):
        ring_copy(i).wait_recv()
        part = part + ring_in[i]
    low_out[...] = part

    def low_copy(i):
        return remote(low_out, low_in.at[i], low_ss.at[i], low_rs.at[i], low_peer(i))

    to_peers(low_copy, reps)

    @pl.when(r != 0)
    def _():
        p_copy(0).wait_recv()

    @pl.when(r == 0)
    def _():
        own_p.wait()

    def gather(j, summed):
        p_copy(j).wait_recv()
        return summed + precv[j].astype(jnp.float32)

    summed = precv[0].astype(jnp.float32)
    for j in range(1, sections):
        summed = gather(j, summed)
    hsend[...] = summed.T.reshape(hsend.shape)

    def h_copy(i):
        peer = rep_peer(i)
        return remote(hsend.at[peer[1]], hrecv.at[i], h_ss.at[i], h_rs.at[i], peer)

    to_peers(h_copy, reps)
    part = low_out[...]
    for i in range(1, reps):
        low_copy(i).wait_recv()
        part = part + low_in[i]
    wall[r] = part

    def g_copy(i):
        return remote(wall.at[r], wall.at[r], g_ss.at[i], g_rs.at[i], rep_peer(i))

    def g_arrival(i):
        source = lax.rem(r - i + reps, reps)
        return remote(wall.at[source], wall.at[source], g_ss.at[i], g_rs.at[i], rep_peer(i))

    to_peers(g_copy, reps)
    rows_grad = hsend[r]
    for i in range(1, reps):
        h_copy(i).wait_recv()
        rows_grad = rows_grad + hrecv[i]
    feat_ref[...] = rows_grad.astype(jnp.bfloat16)
    take(g_arrival, reps)
    wgrad_ref[...] = wall[...].reshape(wgrad_ref.shape)

    @pl.when(r != 0)
    def _():
        x_copy(0).wait_send()
        p_copy(0).wait_send()

    for j in range(1, sections):
        x_copy(j).wait_send()
        p_copy(j).wait_send()
        ring_copy(j).wait_send()
    for i in range(1, reps):
        y_copy(i).wait_send()
        u_copy(i).wait_send()
        w_copy(i).wait_send()
        h_copy(i).wait_send()
        low_copy(i).wait_send()
        g_copy(i).wait_send()


def local(features, weight, tile_vals, tile_pos, tile_count, cotangent):
    reps = lax.axis_size("rep")
    blks = lax.axis_size("blk")
    sections = blks // reps
    rows, feat = features.shape
    hid = weight.shape[1]
    share = rows // reps
    wshare = feat // reps
    adjacency = dense_adjacency(
        tile_vals[0, 0], tile_pos[0, 0], tile_count[0, 0], rows // tile_vals.shape[-1]
    )
    bf, fl = jnp.bfloat16, jnp.float32
    sems = [sections] * 2 + [reps] * 4 + [sections] * 2 + [reps] * 4 + [sections] * 2 + [reps] * 4
    act, feat_grad, weight_grad = pl.pallas_call(
        functools.partial(layer_kernel, blks, reps),
        out_shape=(
            jax.ShapeDtypeStruct((share, hid), bf),
            jax.ShapeDtypeStruct((share, feat), bf),
            jax.ShapeDtypeStruct((feat, hid), fl),
        ),
        in_specs=[pl.BlockSpec(memory_space=pltpu.VMEM)] * 4,
        out_specs=[pl.BlockSpec(memory_space=pltpu.VMEM)] * 3,
        scratch_shapes=[
            pltpu.VMEM((sections, rows, feat), bf),
            pltpu.VMEM((rows, feat), fl),
            pltpu.VMEM((reps, share, feat), fl),
            pltpu.VMEM((reps, share, feat), fl),
            pltpu.VMEM((reps, share, feat), bf),
            pltpu.VMEM((sections, feat, rows), bf),
            pltpu.VMEM((sections, feat, rows), bf),
            pltpu.VMEM((reps, share, feat), fl),
            pltpu.VMEM((reps, share, feat), fl),
            pltpu.VMEM((reps, wshare, hid), fl),
            pltpu.VMEM((reps, wshare, hid), fl),
            pltpu.VMEM((wshare, hid), fl),
            pltpu.VMEM((sections, wshare, hid), fl),
            pltpu.VMEM((wshare, hid), fl),
            pltpu.VMEM((reps, wshare, hid), fl),
            pltpu.VMEM((reps, wshare, hid), fl),
        ]
        + [pltpu.SemaphoreType.DMA((n,)) for n in sems],
        compiler_params=pltpu.CompilerParams(
            collective_id=0, has_side_effects=True, vmem_limit_bytes=48 << 20
        ),
    )(features, weight, adjacency, cotangent)
    return (act, feat_grad, weight_grad)


def solution(mesh):
    placed = (
        P("blk", None),
        P(),
        P("blk", "rep", None, None, None, None),
        P("blk", "rep", None, None),
        P("blk", "rep", None),
        P(("blk", "rep"), None),
    )
    return jax.shard_map(
        local,
        mesh=mesh,
        in_specs=placed,
        out_specs=(P(("blk", "rep"), None), P(("blk", "rep"), None), P()),
        check_vma=False,
    )
```

```python
import functools
import math

import jax
import jax.numpy as jnp
from jax import lax
from jax.experimental import pallas as pl
from jax.experimental.pallas import tpu as pltpu
from jax.sharding import PartitionSpec as P

MESH = pl.DeviceIdType.MESH


def slot_codes(positions, counts, cells):
    slots = jnp.arange(positions.shape[1], dtype=jnp.int32)[None, None, :]
    hits = positions[:, None, :] == jnp.arange(cells, dtype=jnp.int32)[None, :, None]
    hits = hits & (slots < counts[:, None, None])
    return jnp.sum(jnp.where(hits, slots + 1, 0), axis=-1, dtype=jnp.int32)


def gelu_and_slope(value):
    scale = math.sqrt(2.0 / math.pi)
    square = value * value
    bend = jnp.tanh(scale * (value + 0.044715 * (square * value)))
    half = 0.5 * (1.0 + bend)
    slope = half + 0.5 * value * (1.0 - bend * bend) * (
        scale * (1.0 + 3.0 * 0.044715 * square)
    )
    return value * half, slope


def dot(left, right, contract=(1, 0)):
    return lax.dot_general(
        left,
        right,
        (((contract[0],), (contract[1],)), ((), ())),
        preferred_element_type=jnp.float32,
    )


def layer_kernel(
    blks,
    reps,
    features_ref,
    weight_ref,
    tiles_ref,
    code_ref,
    cot_ref,
    act_ref,
    feat_ref,
    wgrad_ref,
    adj_ref,
    xs,
    total,
    ysend,
    yrecv,
    urows,
    kept,
    psend,
    precv,
    hsend,
    hrecv,
    wsend,
    wrecv,
    ring_out,
    ring_in,
    low_out,
    low_in,
    wall,
    x_ss,
    x_rs,
    y_ss,
    y_rs,
    u_ss,
    u_rs,
    p_ss,
    p_rs,
    h_ss,
    h_rs,
    w_ss,
    w_rs,
    ring_ss,
    ring_rs,
    low_ss,
    low_rs,
    g_ss,
    g_rs,
):
    b = lax.axis_index("blk")
    r = lax.axis_index("rep")
    sections = blks // reps
    share = cot_ref.shape[0]
    rows = features_ref.shape[0]

    span = 2 * reps
    turns = sections // 2
    z = lax.div(b, span)
    q = lax.rem(b, span)

    def ahead(s):
        return (z * span + lax.rem(q + r + reps * s, span), r)

    def behind(s):
        return (z * span + lax.rem(q - r - reps * s + 2 * span, span), r)

    up = (lax.rem(z + 1, turns) * span + q, r)
    down = (lax.rem(z + turns - 1, turns) * span + q, r)

    def section_of(g, s):
        wrapped = (q - r - reps * s < 0).astype(jnp.int32)
        return lax.rem(2 * (g - wrapped) + s + sections, sections)

    def rep_peer(i):
        return (b, lax.rem(r + i, reps))

    def ring_peer(i):
        return (lax.rem(b + reps * i, blks), r)

    def low_peer(i):
        low = lax.rem(b, reps)
        return (b - low + lax.rem(low + i, reps), r)

    def remote(src, dst, ss, rs, device):
        return pltpu.make_async_remote_copy(
            src_ref=src,
            dst_ref=dst,
            send_sem=ss,
            recv_sem=rs,
            device_id=device,
            device_id_type=MESH,
        )

    barrier = pltpu.get_barrier_semaphore()

    def greet(device):
        pl.semaphore_signal(barrier, inc=1, device_id=device, device_id_type=MESH)

    @pl.when(r != 0)
    def _():
        greet(ahead(0))
        greet(behind(0))

    greet(ahead(1))
    greet(behind(1))
    greet(up)
    greet(down)
    for j in range(1, sections):
        greet(ring_peer(j))
    for i in range(1, reps):
        greet(rep_peer(i))
        greet(low_peer(i))
    greeted = 4 + (sections - 1) + 2 * (reps - 1)
    pl.semaphore_wait(barrier, jnp.where(r == 0, greeted, greeted + 2))

    def x_copy(g, s):
        at = 2 * g + s
        if g == 0:
            source, device = features_ref, ahead(s)
        elif g == 1:
            source, device = xs.at[s], up
        elif g == 3:
            source, device = xs.at[s], down
        else:
            source, device = xs.at[2 if s == 0 else 7], (up if s == 0 else down)
        return remote(source, xs.at[at], x_ss.at[at], x_rs.at[at], device)

    own_x = pltpu.make_async_copy(features_ref, xs.at[0], x_rs.at[0])

    @pl.when(r != 0)
    def _():
        x_copy(0, 0).start()

    @pl.when(r == 0)
    def _():
        own_x.start()

    x_copy(0, 1).start()

    tile = tiles_ref.shape[-1]
    blocks = rows // tile

    def place(j, carry):
        for n in range(blocks):
            for m in range(blocks):
                code = code_ref[j, n * blocks + m]
                picked = tiles_ref[j, jnp.maximum(code - 1, 0)]
                adj_ref[j, n * tile : (n + 1) * tile, m * tile : (m + 1) * tile] = jnp.where(
                    code > 0, picked, jnp.zeros_like(picked)
                )
        return carry

    lax.fori_loop(0, sections, place, 0)

    @pl.when(r != 0)
    def _():
        x_copy(0, 0).wait_recv()

    @pl.when(r == 0)
    def _():
        own_x.wait()

    x_copy(1, 0).start()
    x_copy(3, 0).start()

    def term(g, s):
        return dot(adj_ref[section_of(g, s)], xs[2 * g + s])

    total[...] = term(0, 0)
    x_copy(0, 1).wait_recv()
    x_copy(3, 1).start()
    x_copy(1, 1).start()
    total[...] += term(0, 1)
    x_copy(1, 0).wait_recv()
    x_copy(2, 0).start()
    total[...] += term(1, 0)
    x_copy(3, 1).wait_recv()
    x_copy(2, 1).start()
    total[...] += term(3, 1)
    for g, s in ((3, 0), (1, 1), (2, 0), (2, 1)):
        x_copy(g, s).wait_recv()
        total[...] += term(g, s)

    ysend[...] = total[...].reshape(reps, share, total.shape[1])

    def to_peers(copy, count):
        for i in range(1, count):
            copy(i).start()

    def take(copy, count):
        for i in range(1, count):
            copy(i).wait_recv()

    def y_copy(i):
        peer = rep_peer(i)
        return remote(ysend.at[peer[1]], yrecv.at[i], y_ss.at[i], y_rs.at[i], peer)

    to_peers(y_copy, reps)
    mixed = ysend[r]
    for i in range(1, reps):
        y_copy(i).wait_recv()
        mixed = mixed + yrecv[i]

    weight = weight_ref[...]
    high = mixed.astype(jnp.bfloat16)
    low = (mixed - high.astype(jnp.float32)).astype(jnp.bfloat16)
    act, slope = gelu_and_slope(dot(high, weight) + dot(low, weight))
    act_ref[...] = act.astype(jnp.bfloat16)
    pre_grad = (cot_ref[...].astype(jnp.float32) * slope).astype(jnp.bfloat16)
    urows[r] = dot(pre_grad, weight, (1, 1)).astype(jnp.bfloat16)

    def u_copy(i):
        return remote(urows.at[r], urows.at[r], u_ss.at[i], u_rs.at[i], rep_peer(i))

    def u_arrival(i):
        source = lax.rem(r - i + reps, reps)
        return remote(urows.at[source], urows.at[source], u_ss.at[i], u_rs.at[i], rep_peer(i))

    to_peers(u_copy, reps)
    wsend[...] = dot(high, pre_grad, (0, 0)).reshape(wsend.shape)

    def w_copy(i):
        peer = rep_peer(i)
        return remote(wsend.at[peer[1]], wrecv.at[i], w_ss.at[i], w_rs.at[i], peer)

    to_peers(w_copy, reps)
    take(u_arrival, reps)
    flipped = urows[...].reshape(rows, urows.shape[2]).T

    def p_copy(at):
        device = (down, up, down, down, up, up, behind(0), behind(1))[at]
        return remote(psend.at[at], precv.at[at], p_ss.at[at], p_rs.at[at], device)

    own_p = pltpu.make_async_copy(psend.at[6], precv.at[6], p_rs.at[6])

    def back(g, s):
        return dot(flipped, adj_ref[section_of(g, s)])

    for at, g, s in ((0, 2, 0), (1, 2, 1), (3, 1, 1), (4, 3, 0)):
        psend[at] = back(g, s).astype(jnp.bfloat16)
        p_copy(at).start()
    kept[0] = back(0, 0)
    kept[1] = back(0, 1)
    for near, at, g, s in ((0, 2, 1, 0), (1, 5, 3, 1)):
        mine = back(g, s)
        p_copy(near).wait_recv()
        psend[at] = (mine + precv[near].astype(jnp.float32)).astype(jnp.bfloat16)
        p_copy(at).start()

    part = wsend[r]
    for i in range(1, reps):
        w_copy(i).wait_recv()
        part = part + wrecv[i]
    ring_out[...] = part

    def ring_copy(i):
        return remote(ring_out, ring_in.at[i], ring_ss.at[i], ring_rs.at[i], ring_peer(i))

    to_peers(ring_copy, sections)
    for s in (1, 0):
        far, near = (3, 5) if s == 1 else (2, 4)
        p_copy(far).wait_recv()
        p_copy(near).wait_recv()
        psend[6 + s] = (
            kept[s] + precv[far].astype(jnp.float32) + precv[near].astype(jnp.float32)
        ).astype(jnp.bfloat16)
        if s == 1:
            p_copy(7).start()

    @pl.when(r != 0)
    def _():
        p_copy(6).start()

    @pl.when(r == 0)
    def _():
        own_p.start()

    for i in range(1, sections):
        ring_copy(i).wait_recv()
        part = part + ring_in[i]
    low_out[...] = part

    def low_copy(i):
        return remote(low_out, low_in.at[i], low_ss.at[i], low_rs.at[i], low_peer(i))

    to_peers(low_copy, reps)

    @pl.when(r != 0)
    def _():
        p_copy(6).wait_recv()

    @pl.when(r == 0)
    def _():
        own_p.wait()

    p_copy(7).wait_recv()
    summed = precv[6].astype(jnp.float32) + precv[7].astype(jnp.float32)
    hsend[...] = summed.T.reshape(hsend.shape)

    def h_copy(i):
        peer = rep_peer(i)
        return remote(hsend.at[peer[1]], hrecv.at[i], h_ss.at[i], h_rs.at[i], peer)

    to_peers(h_copy, reps)
    part = low_out[...]
    for i in range(1, reps):
        low_copy(i).wait_recv()
        part = part + low_in[i]
    wall[r] = part

    def g_copy(i):
        return remote(wall.at[r], wall.at[r], g_ss.at[i], g_rs.at[i], rep_peer(i))

    def g_arrival(i):
        source = lax.rem(r - i + reps, reps)
        return remote(wall.at[source], wall.at[source], g_ss.at[i], g_rs.at[i], rep_peer(i))

    to_peers(g_copy, reps)
    rows_grad = hsend[r]
    for i in range(1, reps):
        h_copy(i).wait_recv()
        rows_grad = rows_grad + hrecv[i]
    feat_ref[...] = rows_grad.astype(jnp.bfloat16)
    take(g_arrival, reps)
    wgrad_ref[...] = wall[...].reshape(wgrad_ref.shape)

    @pl.when(r != 0)
    def _():
        x_copy(0, 0).wait_send()
        p_copy(6).wait_send()

    x_copy(0, 1).wait_send()
    for g in range(1, 4):
        x_copy(g, 0).wait_send()
        x_copy(g, 1).wait_send()
    for at in (0, 1, 2, 3, 4, 5, 7):
        p_copy(at).wait_send()
    for j in range(1, sections):
        ring_copy(j).wait_send()
    for i in range(1, reps):
        y_copy(i).wait_send()
        u_copy(i).wait_send()
        w_copy(i).wait_send()
        h_copy(i).wait_send()
        low_copy(i).wait_send()
        g_copy(i).wait_send()


def local(features, weight, tile_vals, tile_pos, tile_count, cotangent):
    reps = lax.axis_size("rep")
    blks = lax.axis_size("blk")
    sections = blks // reps
    rows, feat = features.shape
    hid = weight.shape[1]
    share = rows // reps
    wshare = feat // reps
    blocks = rows // tile_vals.shape[-1]
    codes = slot_codes(tile_pos[0, 0], tile_count[0, 0], blocks * blocks)
    bf, fl = jnp.bfloat16, jnp.float32
    sems = [sections] * 2 + [reps] * 4 + [sections] * 2 + [reps] * 4 + [sections] * 2 + [reps] * 4
    act, feat_grad, weight_grad = pl.pallas_call(
        functools.partial(layer_kernel, blks, reps),
        out_shape=(
            jax.ShapeDtypeStruct((share, hid), bf),
            jax.ShapeDtypeStruct((share, feat), bf),
            jax.ShapeDtypeStruct((feat, hid), fl),
        ),
        in_specs=[pl.BlockSpec(memory_space=pltpu.VMEM)] * 3
        + [pl.BlockSpec(memory_space=pltpu.SMEM), pl.BlockSpec(memory_space=pltpu.VMEM)],
        out_specs=[pl.BlockSpec(memory_space=pltpu.VMEM)] * 3,
        scratch_shapes=[
            pltpu.VMEM((sections, rows, rows), bf),
            pltpu.VMEM((sections, rows, feat), bf),
            pltpu.VMEM((rows, feat), fl),
            pltpu.VMEM((reps, share, feat), fl),
            pltpu.VMEM((reps, share, feat), fl),
            pltpu.VMEM((reps, share, feat), bf),
            pltpu.VMEM((2, feat, rows), fl),
            pltpu.VMEM((sections, feat, rows), bf),
            pltpu.VMEM((sections, feat, rows), bf),
            pltpu.VMEM((reps, share, feat), fl),
            pltpu.VMEM((reps, share, feat), fl),
            pltpu.VMEM((reps, wshare, hid), fl),
            pltpu.VMEM((reps, wshare, hid), fl),
            pltpu.VMEM((wshare, hid), fl),
            pltpu.VMEM((sections, wshare, hid), fl),
            pltpu.VMEM((wshare, hid), fl),
            pltpu.VMEM((reps, wshare, hid), fl),
            pltpu.VMEM((reps, wshare, hid), fl),
        ]
        + [pltpu.SemaphoreType.DMA((n,)) for n in sems],
        compiler_params=pltpu.CompilerParams(
            collective_id=0, has_side_effects=True, vmem_limit_bytes=48 << 20
        ),
    )(features, weight, tile_vals[0, 0], codes, cotangent)
    return (act, feat_grad, weight_grad)


def solution(mesh):
    placed = (
        P("blk", None),
        P(),
        P("blk", "rep", None, None, None, None),
        P("blk", "rep", None, None),
        P("blk", "rep", None),
        P(("blk", "rep"), None),
    )
    return jax.shard_map(
        local,
        mesh=mesh,
        in_specs=placed,
        out_specs=(P(("blk", "rep"), None), P(("blk", "rep"), None), P()),
        check_vma=False,
    )
```

```python
import functools
import math

import jax
import jax.numpy as jnp
from jax import lax
from jax.experimental import pallas as pl
from jax.experimental.pallas import tpu as pltpu
from jax.sharding import PartitionSpec as P

MESH = pl.DeviceIdType.MESH


def slot_codes(positions, counts, cells):
    slots = jnp.arange(positions.shape[1], dtype=jnp.int32)[None, None, :]
    hits = positions[:, None, :] == jnp.arange(cells, dtype=jnp.int32)[None, :, None]
    hits = hits & (slots < counts[:, None, None])
    return jnp.sum(jnp.where(hits, slots + 1, 0), axis=-1, dtype=jnp.int32)


def gelu_and_slope(value):
    scale = math.sqrt(2.0 / math.pi)
    square = value * value
    bend = jnp.tanh(scale * (value + 0.044715 * (square * value)))
    half = 0.5 * (1.0 + bend)
    slope = half + 0.5 * value * (1.0 - bend * bend) * (
        scale * (1.0 + 3.0 * 0.044715 * square)
    )
    return value * half, slope


def dot(left, right, contract=(1, 0)):
    return lax.dot_general(
        left,
        right,
        (((contract[0],), (contract[1],)), ((), ())),
        preferred_element_type=jnp.float32,
    )


def layer_kernel(
    blks,
    reps,
    features_ref,
    weight_ref,
    tiles_ref,
    code_ref,
    cot_ref,
    act_ref,
    feat_ref,
    wgrad_ref,
    adj_ref,
    xs,
    total,
    ysend,
    yrecv,
    urows,
    kept,
    psend,
    precv,
    hsend,
    hrecv,
    wsend,
    wrecv,
    q_out,
    q_in,
    z_out,
    z_in,
    wall,
    x_ss,
    x_rs,
    y_ss,
    y_rs,
    u_ss,
    u_rs,
    p_ss,
    p_rs,
    h_ss,
    h_rs,
    w_ss,
    w_rs,
    q_ss,
    q_rs,
    z_ss,
    z_rs,
    g_ss,
    g_rs,
):
    b = lax.axis_index("blk")
    r = lax.axis_index("rep")
    sections = blks // reps
    share = cot_ref.shape[0]
    rows = features_ref.shape[0]

    span = 2 * reps
    turns = sections // 2
    z = lax.div(b, span)
    q = lax.rem(b, span)

    def ahead(s):
        return (z * span + lax.rem(q + r + reps * s, span), r)

    def behind(s):
        return (z * span + lax.rem(q - r - reps * s + 2 * span, span), r)

    up = (lax.rem(z + 1, turns) * span + q, r)
    down = (lax.rem(z + turns - 1, turns) * span + q, r)

    def section_of(g, s):
        wrapped = (q - r - reps * s < 0).astype(jnp.int32)
        return lax.rem(2 * (g - wrapped) + s + sections, sections)

    def rep_peer(i):
        return (b, lax.rem(r + i, reps))

    def q_peer(i):
        return (z * span + lax.rem(q + i, span), r)

    def z_peer(i):
        return (lax.rem(z + i, turns) * span + q, r)

    def remote(src, dst, ss, rs, device):
        return pltpu.make_async_remote_copy(
            src_ref=src,
            dst_ref=dst,
            send_sem=ss,
            recv_sem=rs,
            device_id=device,
            device_id_type=MESH,
        )

    barrier = pltpu.get_barrier_semaphore()

    def greet(device):
        pl.semaphore_signal(barrier, inc=1, device_id=device, device_id_type=MESH)

    @pl.when(r != 0)
    def _():
        greet(ahead(0))
        greet(behind(0))

    greet(ahead(1))
    greet(behind(1))
    greet(up)
    greet(down)
    for i in range(1, turns):
        greet(z_peer(i))
    for i in range(1, span):
        greet(q_peer(i))
    for i in range(1, reps):
        greet(rep_peer(i))
    greeted = 4 + (turns - 1) + (span - 1) + (reps - 1)
    pl.semaphore_wait(barrier, jnp.where(r == 0, greeted, greeted + 2))

    part_rows = rows // 2

    def x_copy(g, s, c):
        at = 2 * g + s
        piece = pl.ds(c * part_rows, part_rows)
        if g == 0:
            source, device = features_ref, ahead(s)
        elif g == 1:
            source, device = xs.at[s], up
        elif g == 3:
            source, device = xs.at[s], down
        else:
            source, device = xs.at[2 if s == 0 else 7], (up if s == 0 else down)
        return remote(
            source.at[piece], xs.at[at, piece], x_ss.at[at, c], x_rs.at[at, c], device
        )

    def own_x(c):
        piece = pl.ds(c * part_rows, part_rows)
        return pltpu.make_async_copy(features_ref.at[piece], xs.at[0, piece], x_rs.at[0, c])

    for c in range(2):

        @pl.when(r != 0)
        def _():
            x_copy(0, 0, c).start()

        @pl.when(r == 0)
        def _():
            own_x(c).start()

        x_copy(0, 1, c).start()

    tile = tiles_ref.shape[-1]
    blocks = rows // tile

    def place(j, carry):
        for n in range(blocks):
            for m in range(blocks):
                code = code_ref[j, n * blocks + m]
                picked = tiles_ref[j, jnp.maximum(code - 1, 0)]
                adj_ref[j, n * tile : (n + 1) * tile, m * tile : (m + 1) * tile] = jnp.where(
                    code > 0, picked, jnp.zeros_like(picked)
                )
        return carry

    lax.fori_loop(0, sections, place, 0)

    def term(g, s):
        return dot(adj_ref[section_of(g, s)], xs[2 * g + s])

    for c in range(2):

        @pl.when(r != 0)
        def _():
            x_copy(0, 0, c).wait_recv()

        @pl.when(r == 0)
        def _():
            own_x(c).wait()

        x_copy(1, 0, c).start()
        x_copy(3, 0, c).start()
        x_copy(0, 1, c).wait_recv()
        x_copy(3, 1, c).start()
        x_copy(1, 1, c).start()

    total[...] = term(0, 0) + term(0, 1)
    for c in range(2):
        x_copy(1, 0, c).wait_recv()
        x_copy(2, 0, c).start()
        x_copy(3, 1, c).wait_recv()
        x_copy(2, 1, c).start()
    total[...] += term(1, 0) + term(3, 1)
    for g, s in ((3, 0), (1, 1), (2, 0), (2, 1)):
        x_copy(g, s, 0).wait_recv()
        x_copy(g, s, 1).wait_recv()
        total[...] += term(g, s)

    ysend[...] = total[...].astype(jnp.bfloat16).reshape(ysend.shape)

    def to_peers(copy, count):
        for i in range(1, count):
            copy(i).start()

    def take(copy, count):
        for i in range(1, count):
            copy(i).wait_recv()

    def y_copy(i):
        peer = rep_peer(i)
        return remote(ysend.at[peer[1]], yrecv.at[i], y_ss.at[i], y_rs.at[i], peer)

    to_peers(y_copy, reps)
    mixed = ysend[r].astype(jnp.float32)
    for i in range(1, reps):
        y_copy(i).wait_recv()
        mixed = mixed + yrecv[i].astype(jnp.float32)

    weight = weight_ref[...]
    high = mixed.astype(jnp.bfloat16)
    low = (mixed - high.astype(jnp.float32)).astype(jnp.bfloat16)
    act, slope = gelu_and_slope(dot(high, weight) + dot(low, weight))
    act_ref[...] = act.astype(jnp.bfloat16)
    pre_grad = (cot_ref[...].astype(jnp.float32) * slope).astype(jnp.bfloat16)
    urows[r] = dot(pre_grad, weight, (1, 1)).astype(jnp.bfloat16)

    def u_copy(i):
        return remote(urows.at[r], urows.at[r], u_ss.at[i], u_rs.at[i], rep_peer(i))

    def u_arrival(i):
        source = lax.rem(r - i + reps, reps)
        return remote(urows.at[source], urows.at[source], u_ss.at[i], u_rs.at[i], rep_peer(i))

    to_peers(u_copy, reps)
    wsend[...] = dot(high, pre_grad, (0, 0)).reshape(wsend.shape)

    def w_copy(i):
        peer = rep_peer(i)
        return remote(wsend.at[peer[1]], wrecv.at[i], w_ss.at[i], w_rs.at[i], peer)

    to_peers(w_copy, reps)
    take(u_arrival, reps)
    flipped = urows[...].reshape(rows, urows.shape[2]).T

    def p_copy(at, c):
        device = (down, up, down, down, up, up, behind(0), behind(1))[at]
        return remote(psend.at[at, c], precv.at[at, c], p_ss.at[at, c], p_rs.at[at, c], device)

    def own_p(c):
        return pltpu.make_async_copy(psend.at[6, c], precv.at[6, c], p_rs.at[6, c])

    def back(g, s):
        return dot(flipped, adj_ref[section_of(g, s)])

    def half(value, c):
        return value[:, c * part_rows : (c + 1) * part_rows]

    def arrived(at, c):
        p_copy(at, c).wait_recv()
        return precv[at, c].astype(jnp.float32)

    for pair in (((0, 2, 0), (1, 2, 1)), ((3, 1, 1), (4, 3, 0))):
        for at, g, s in pair:
            value = back(g, s).astype(jnp.bfloat16)
            psend[at, 0] = half(value, 0)
            psend[at, 1] = half(value, 1)
            p_copy(at, 0).start()
            p_copy(at, 1).start()
    for at, g, s in ((0, 0, 0), (1, 0, 1), (2, 1, 0), (3, 3, 1)):
        kept[at] = back(g, s)

    part = wsend[r]
    for i in range(1, reps):
        w_copy(i).wait_recv()
        part = part + wrecv[i]
    q_out[...] = part

    def q_copy(i):
        return remote(q_out, q_in.at[i], q_ss.at[i], q_rs.at[i], q_peer(i))

    to_peers(q_copy, span)

    for c in range(2):
        for near, at in ((0, 2), (1, 5)):
            mine = half(kept[2 + near], c)
            psend[at, c] = (mine + arrived(near, c)).astype(jnp.bfloat16)
            p_copy(at, c).start()

    for i in range(1, span):
        q_copy(i).wait_recv()
        part = part + q_in[i]
    z_out[...] = part

    def z_copy(i):
        return remote(z_out, z_in.at[i], z_ss.at[i], z_rs.at[i], z_peer(i))

    to_peers(z_copy, turns)

    for c in range(2):
        psend[7, c] = (half(kept[1], c) + arrived(3, c) + arrived(5, c)).astype(jnp.bfloat16)
        p_copy(7, c).start()
        psend[6, c] = (half(kept[0], c) + arrived(2, c) + arrived(4, c)).astype(jnp.bfloat16)

        @pl.when(r != 0)
        def _():
            p_copy(6, c).start()

        @pl.when(r == 0)
        def _():
            own_p(c).start()

    for i in range(1, turns):
        z_copy(i).wait_recv()
        part = part + z_in[i]
    wall[r] = part

    def g_copy(i):
        return remote(wall.at[r], wall.at[r], g_ss.at[i], g_rs.at[i], rep_peer(i))

    def g_arrival(i):
        source = lax.rem(r - i + reps, reps)
        return remote(wall.at[source], wall.at[source], g_ss.at[i], g_rs.at[i], rep_peer(i))

    to_peers(g_copy, reps)

    def owned(c):
        @pl.when(r != 0)
        def _():
            p_copy(6, c).wait_recv()

        @pl.when(r == 0)
        def _():
            own_p(c).wait()

        return precv[6, c].astype(jnp.float32) + arrived(7, c)

    for c in range(2):
        kept[0, :, c * part_rows : (c + 1) * part_rows] = owned(c)
    summed = kept[0]
    hsend[...] = summed.T.astype(jnp.bfloat16).reshape(hsend.shape)

    def h_copy(i):
        peer = rep_peer(i)
        return remote(hsend.at[peer[1]], hrecv.at[i], h_ss.at[i], h_rs.at[i], peer)

    to_peers(h_copy, reps)
    rows_grad = hsend[r].astype(jnp.float32)
    for i in range(1, reps):
        h_copy(i).wait_recv()
        rows_grad = rows_grad + hrecv[i].astype(jnp.float32)
    feat_ref[...] = rows_grad.astype(jnp.bfloat16)
    take(g_arrival, reps)
    wgrad_ref[...] = wall[...].reshape(wgrad_ref.shape)

    for c in range(2):

        @pl.when(r != 0)
        def _():
            x_copy(0, 0, c).wait_send()
            p_copy(6, c).wait_send()

        x_copy(0, 1, c).wait_send()
        for g in range(1, 4):
            x_copy(g, 0, c).wait_send()
            x_copy(g, 1, c).wait_send()
        for at in (0, 1, 2, 3, 4, 5, 7):
            p_copy(at, c).wait_send()
    for i in range(1, turns):
        z_copy(i).wait_send()
    for i in range(1, span):
        q_copy(i).wait_send()
    for i in range(1, reps):
        y_copy(i).wait_send()
        u_copy(i).wait_send()
        w_copy(i).wait_send()
        h_copy(i).wait_send()
        g_copy(i).wait_send()


def local(features, weight, tile_vals, tile_pos, tile_count, cotangent):
    reps = lax.axis_size("rep")
    blks = lax.axis_size("blk")
    sections = blks // reps
    rows, feat = features.shape
    hid = weight.shape[1]
    share = rows // reps
    wshare = feat // reps
    blocks = rows // tile_vals.shape[-1]
    codes = slot_codes(tile_pos[0, 0], tile_count[0, 0], blocks * blocks)
    bf, fl = jnp.bfloat16, jnp.float32
    span, turns = 2 * reps, sections // 2
    halves = (sections, 2)
    sems = [halves] * 2 + [(reps,)] * 4 + [halves] * 2 + [(reps,)] * 4
    sems += [(span,)] * 2 + [(turns,)] * 2 + [(reps,)] * 2
    act, feat_grad, weight_grad = pl.pallas_call(
        functools.partial(layer_kernel, blks, reps),
        out_shape=(
            jax.ShapeDtypeStruct((share, hid), bf),
            jax.ShapeDtypeStruct((share, feat), bf),
            jax.ShapeDtypeStruct((feat, hid), fl),
        ),
        in_specs=[pl.BlockSpec(memory_space=pltpu.VMEM)] * 3
        + [pl.BlockSpec(memory_space=pltpu.SMEM), pl.BlockSpec(memory_space=pltpu.VMEM)],
        out_specs=[pl.BlockSpec(memory_space=pltpu.VMEM)] * 3,
        scratch_shapes=[
            pltpu.VMEM((sections, rows, rows), bf),
            pltpu.VMEM((sections, rows, feat), bf),
            pltpu.VMEM((rows, feat), fl),
            pltpu.VMEM((reps, share, feat), bf),
            pltpu.VMEM((reps, share, feat), bf),
            pltpu.VMEM((reps, share, feat), bf),
            pltpu.VMEM((4, feat, rows), fl),
            pltpu.VMEM((sections, 2, feat, rows // 2), bf),
            pltpu.VMEM((sections, 2, feat, rows // 2), bf),
            pltpu.VMEM((reps, share, feat), bf),
            pltpu.VMEM((reps, share, feat), bf),
            pltpu.VMEM((reps, wshare, hid), fl),
            pltpu.VMEM((reps, wshare, hid), fl),
            pltpu.VMEM((wshare, hid), fl),
            pltpu.VMEM((span, wshare, hid), fl),
            pltpu.VMEM((wshare, hid), fl),
            pltpu.VMEM((turns, wshare, hid), fl),
            pltpu.VMEM((reps, wshare, hid), fl),
        ]
        + [pltpu.SemaphoreType.DMA(shape) for shape in sems],
        compiler_params=pltpu.CompilerParams(
            collective_id=0, has_side_effects=True, vmem_limit_bytes=48 << 20
        ),
    )(features, weight, tile_vals[0, 0], codes, cotangent)
    return (act, feat_grad, weight_grad)


def solution(mesh):
    placed = (
        P("blk", None),
        P(),
        P("blk", "rep", None, None, None, None),
        P("blk", "rep", None, None),
        P("blk", "rep", None),
        P(("blk", "rep"), None),
    )
    return jax.shard_map(
        local,
        mesh=mesh,
        in_specs=placed,
        out_specs=(P(("blk", "rep"), None), P(("blk", "rep"), None), P()),
        check_vma=False,
    )
```

```python
import functools
import math

import jax
import jax.numpy as jnp
from jax import lax
from jax.experimental import pallas as pl
from jax.experimental.pallas import tpu as pltpu
from jax.sharding import PartitionSpec as P

MESH = pl.DeviceIdType.MESH


def slot_codes(positions, counts, cells):
    slots = jnp.arange(positions.shape[1], dtype=jnp.int32)[None, None, :]
    hits = positions[:, None, :] == jnp.arange(cells, dtype=jnp.int32)[None, :, None]
    hits = hits & (slots < counts[:, None, None])
    return jnp.sum(jnp.where(hits, slots + 1, 0), axis=-1, dtype=jnp.int32)


def gelu_and_slope(value):
    scale = math.sqrt(2.0 / math.pi)
    square = value * value
    bend = jnp.tanh(scale * (value + 0.044715 * (square * value)))
    half = 0.5 * (1.0 + bend)
    slope = half + 0.5 * value * (1.0 - bend * bend) * (
        scale * (1.0 + 3.0 * 0.044715 * square)
    )
    return value * half, slope


def dot(left, right, contract=(1, 0)):
    return lax.dot_general(
        left,
        right,
        (((contract[0],), (contract[1],)), ((), ())),
        preferred_element_type=jnp.float32,
    )


def layer_kernel(
    blks,
    reps,
    features_ref,
    weight_hbm,
    tiles_hbm,
    code_ref,
    cot_hbm,
    act_ref,
    feat_ref,
    wgrad_ref,
    weight_ref,
    tiles_ref,
    cot_ref,
    adj_ref,
    xs,
    total,
    ysend,
    yrecv,
    urows,
    kept,
    psend,
    precv,
    hsend,
    hrecv,
    wsend,
    wrecv,
    q_out,
    q_in,
    z_out,
    z_in,
    wall,
    load_sems,
    x_ss,
    x_rs,
    y_ss,
    y_rs,
    u_ss,
    u_rs,
    p_ss,
    p_rs,
    h_ss,
    h_rs,
    w_ss,
    w_rs,
    q_ss,
    q_rs,
    z_ss,
    z_rs,
    g_ss,
    g_rs,
):
    b = lax.axis_index("blk")
    r = lax.axis_index("rep")
    sections = blks // reps
    share = cot_ref.shape[0]
    rows = features_ref.shape[0]

    span = 2 * reps
    turns = sections // 2
    z = lax.div(b, span)
    q = lax.rem(b, span)

    def ahead(s):
        return (z * span + lax.rem(q + r + reps * s, span), r)

    def behind(s):
        return (z * span + lax.rem(q - r - reps * s + 2 * span, span), r)

    up = (lax.rem(z + 1, turns) * span + q, r)
    down = (lax.rem(z + turns - 1, turns) * span + q, r)

    def section_of(g, s):
        wrapped = (q - r - reps * s < 0).astype(jnp.int32)
        return lax.rem(2 * (g - wrapped) + s + sections, sections)

    def rep_peer(i):
        return (b, lax.rem(r + i, reps))

    def q_peer(i):
        return (z * span + lax.rem(q + i, span), r)

    def z_peer(i):
        return (lax.rem(z + i, turns) * span + q, r)

    def remote(src, dst, ss, rs, device):
        return pltpu.make_async_remote_copy(
            src_ref=src,
            dst_ref=dst,
            send_sem=ss,
            recv_sem=rs,
            device_id=device,
            device_id_type=MESH,
        )

    loads = [
        pltpu.make_async_copy(source, target, load_sems.at[i])
        for i, (source, target) in enumerate(
            ((tiles_hbm, tiles_ref), (weight_hbm, weight_ref), (cot_hbm, cot_ref))
        )
    ]
    for load in loads:
        load.start()

    barrier = pltpu.get_barrier_semaphore()

    def greet(device):
        pl.semaphore_signal(barrier, inc=1, device_id=device, device_id_type=MESH)

    @pl.when(r != 0)
    def _():
        greet(ahead(0))
        greet(behind(0))

    greet(ahead(1))
    greet(behind(1))
    greet(up)
    greet(down)
    for i in range(1, turns):
        greet(z_peer(i))
    for i in range(1, span):
        greet(q_peer(i))
    for i in range(1, reps):
        greet(rep_peer(i))
    greeted = 4 + (turns - 1) + (span - 1) + (reps - 1)
    pl.semaphore_wait(barrier, jnp.where(r == 0, greeted, greeted + 2))

    part_rows = rows // 2

    def x_copy(g, s, c):
        at = 2 * g + s
        piece = pl.ds(c * part_rows, part_rows)
        if g == 0:
            source, device = features_ref, ahead(s)
        elif g == 1:
            source, device = xs.at[s], up
        elif g == 3:
            source, device = xs.at[s], down
        else:
            source, device = xs.at[2 if s == 0 else 7], (up if s == 0 else down)
        return remote(
            source.at[piece], xs.at[at, piece], x_ss.at[at, c], x_rs.at[at, c], device
        )

    def own_x(c):
        piece = pl.ds(c * part_rows, part_rows)
        return pltpu.make_async_copy(features_ref.at[piece], xs.at[0, piece], x_rs.at[0, c])

    for c in range(2):

        @pl.when(r != 0)
        def _():
            x_copy(0, 0, c).start()

        @pl.when(r == 0)
        def _():
            own_x(c).start()

        x_copy(0, 1, c).start()

    tile = tiles_ref.shape[-1]
    blocks = rows // tile

    def place(j, carry):
        for n in range(blocks):
            for m in range(blocks):
                code = code_ref[j, n * blocks + m]
                picked = tiles_ref[j, jnp.maximum(code - 1, 0)]
                adj_ref[j, n * tile : (n + 1) * tile, m * tile : (m + 1) * tile] = jnp.where(
                    code > 0, picked, jnp.zeros_like(picked)
                )
        return carry

    loads[0].wait()
    lax.fori_loop(0, sections, place, 0)
    loads[1].wait()
    loads[2].wait()

    def term(g, s):
        return dot(adj_ref[section_of(g, s)], xs[2 * g + s])

    for c in range(2):

        @pl.when(r != 0)
        def _():
            x_copy(0, 0, c).wait_recv()

        @pl.when(r == 0)
        def _():
            own_x(c).wait()

        x_copy(1, 0, c).start()
        x_copy(3, 0, c).start()
        x_copy(0, 1, c).wait_recv()
        x_copy(3, 1, c).start()
        x_copy(1, 1, c).start()

    total[...] = term(0, 0) + term(0, 1)
    for c in range(2):
        x_copy(1, 0, c).wait_recv()
        x_copy(2, 0, c).start()
        x_copy(3, 1, c).wait_recv()
        x_copy(2, 1, c).start()
    total[...] += term(1, 0) + term(3, 1)
    for g, s in ((3, 0), (1, 1), (2, 0), (2, 1)):
        x_copy(g, s, 0).wait_recv()
        x_copy(g, s, 1).wait_recv()
        total[...] += term(g, s)

    ysend[...] = total[...].astype(jnp.bfloat16).reshape(ysend.shape)

    def to_peers(copy, count):
        for i in range(1, count):
            copy(i).start()

    def take(copy, count):
        for i in range(1, count):
            copy(i).wait_recv()

    def y_copy(i):
        peer = rep_peer(i)
        return remote(ysend.at[peer[1]], yrecv.at[i], y_ss.at[i], y_rs.at[i], peer)

    to_peers(y_copy, reps)
    mixed = ysend[r].astype(jnp.float32)
    for i in range(1, reps):
        y_copy(i).wait_recv()
        mixed = mixed + yrecv[i].astype(jnp.float32)

    weight = weight_ref[...]
    high = mixed.astype(jnp.bfloat16)
    low = (mixed - high.astype(jnp.float32)).astype(jnp.bfloat16)
    act, slope = gelu_and_slope(dot(high, weight) + dot(low, weight))
    act_ref[...] = act.astype(jnp.bfloat16)
    pre_grad = (cot_ref[...].astype(jnp.float32) * slope).astype(jnp.bfloat16)
    urows[r] = dot(pre_grad, weight, (1, 1)).astype(jnp.bfloat16)

    def u_copy(i):
        return remote(urows.at[r], urows.at[r], u_ss.at[i], u_rs.at[i], rep_peer(i))

    def u_arrival(i):
        source = lax.rem(r - i + reps, reps)
        return remote(urows.at[source], urows.at[source], u_ss.at[i], u_rs.at[i], rep_peer(i))

    to_peers(u_copy, reps)
    wsend[...] = dot(high, pre_grad, (0, 0)).reshape(wsend.shape)

    def w_copy(i):
        peer = rep_peer(i)
        return remote(wsend.at[peer[1]], wrecv.at[i], w_ss.at[i], w_rs.at[i], peer)

    to_peers(w_copy, reps)
    take(u_arrival, reps)
    flipped = urows[...].reshape(rows, urows.shape[2]).T

    def p_copy(at, c):
        device = (down, up, down, down, up, up, behind(0), behind(1))[at]
        return remote(psend.at[at, c], precv.at[at, c], p_ss.at[at, c], p_rs.at[at, c], device)

    def own_p(c):
        return pltpu.make_async_copy(psend.at[6, c], precv.at[6, c], p_rs.at[6, c])

    def back(g, s):
        return dot(flipped, adj_ref[section_of(g, s)])

    def half(value, c):
        return value[:, c * part_rows : (c + 1) * part_rows]

    def arrived(at, c):
        p_copy(at, c).wait_recv()
        return precv[at, c].astype(jnp.float32)

    for pair in (((0, 2, 0), (1, 2, 1)), ((3, 1, 1), (4, 3, 0))):
        for at, g, s in pair:
            value = back(g, s).astype(jnp.bfloat16)
            psend[at, 0] = half(value, 0)
            psend[at, 1] = half(value, 1)
            p_copy(at, 0).start()
            p_copy(at, 1).start()
    for at, g, s in ((0, 0, 0), (1, 0, 1), (2, 1, 0), (3, 3, 1)):
        kept[at] = back(g, s)

    part = wsend[r]
    for i in range(1, reps):
        w_copy(i).wait_recv()
        part = part + wrecv[i]
    q_out[...] = part

    def q_copy(i):
        return remote(q_out, q_in.at[i], q_ss.at[i], q_rs.at[i], q_peer(i))

    to_peers(q_copy, span)

    for c in range(2):
        for near, at in ((0, 2), (1, 5)):
            mine = half(kept[2 + near], c)
            psend[at, c] = (mine + arrived(near, c)).astype(jnp.bfloat16)
            p_copy(at, c).start()

    for i in range(1, span):
        q_copy(i).wait_recv()
        part = part + q_in[i]
    z_out[...] = part

    def z_copy(i):
        return remote(z_out, z_in.at[i], z_ss.at[i], z_rs.at[i], z_peer(i))

    to_peers(z_copy, turns)

    for c in range(2):
        psend[7, c] = (half(kept[1], c) + arrived(3, c) + arrived(5, c)).astype(jnp.bfloat16)
        p_copy(7, c).start()
        psend[6, c] = (half(kept[0], c) + arrived(2, c) + arrived(4, c)).astype(jnp.bfloat16)

        @pl.when(r != 0)
        def _():
            p_copy(6, c).start()

        @pl.when(r == 0)
        def _():
            own_p(c).start()

    for i in range(1, turns):
        z_copy(i).wait_recv()
        part = part + z_in[i]
    wall[r] = part

    def g_copy(i):
        return remote(wall.at[r], wall.at[r], g_ss.at[i], g_rs.at[i], rep_peer(i))

    def g_arrival(i):
        source = lax.rem(r - i + reps, reps)
        return remote(wall.at[source], wall.at[source], g_ss.at[i], g_rs.at[i], rep_peer(i))

    to_peers(g_copy, reps)

    def owned(c):
        @pl.when(r != 0)
        def _():
            p_copy(6, c).wait_recv()

        @pl.when(r == 0)
        def _():
            own_p(c).wait()

        return precv[6, c].astype(jnp.float32) + arrived(7, c)

    for c in range(2):
        kept[0, :, c * part_rows : (c + 1) * part_rows] = owned(c)
    summed = kept[0]
    hsend[...] = summed.T.astype(jnp.bfloat16).reshape(hsend.shape)

    def h_copy(i):
        peer = rep_peer(i)
        return remote(hsend.at[peer[1]], hrecv.at[i], h_ss.at[i], h_rs.at[i], peer)

    to_peers(h_copy, reps)
    rows_grad = hsend[r].astype(jnp.float32)
    for i in range(1, reps):
        h_copy(i).wait_recv()
        rows_grad = rows_grad + hrecv[i].astype(jnp.float32)
    feat_ref[...] = rows_grad.astype(jnp.bfloat16)
    take(g_arrival, reps)
    wgrad_ref[...] = wall[...].reshape(wgrad_ref.shape)

    for c in range(2):

        @pl.when(r != 0)
        def _():
            x_copy(0, 0, c).wait_send()
            p_copy(6, c).wait_send()

        x_copy(0, 1, c).wait_send()
        for g in range(1, 4):
            x_copy(g, 0, c).wait_send()
            x_copy(g, 1, c).wait_send()
        for at in (0, 1, 2, 3, 4, 5, 7):
            p_copy(at, c).wait_send()
    for i in range(1, turns):
        z_copy(i).wait_send()
    for i in range(1, span):
        q_copy(i).wait_send()
    for i in range(1, reps):
        y_copy(i).wait_send()
        u_copy(i).wait_send()
        w_copy(i).wait_send()
        h_copy(i).wait_send()
        g_copy(i).wait_send()


def local(features, weight, tile_vals, tile_pos, tile_count, cotangent):
    reps = lax.axis_size("rep")
    blks = lax.axis_size("blk")
    sections = blks // reps
    rows, feat = features.shape
    hid = weight.shape[1]
    share = rows // reps
    wshare = feat // reps
    blocks = rows // tile_vals.shape[-1]
    codes = slot_codes(tile_pos[0, 0], tile_count[0, 0], blocks * blocks)
    bf, fl = jnp.bfloat16, jnp.float32
    span, turns = 2 * reps, sections // 2
    halves = (sections, 2)
    sems = [(3,)] + [halves] * 2 + [(reps,)] * 4 + [halves] * 2 + [(reps,)] * 4
    sems += [(span,)] * 2 + [(turns,)] * 2 + [(reps,)] * 2
    act, feat_grad, weight_grad = pl.pallas_call(
        functools.partial(layer_kernel, blks, reps),
        out_shape=(
            jax.ShapeDtypeStruct((share, hid), bf),
            jax.ShapeDtypeStruct((share, feat), bf),
            jax.ShapeDtypeStruct((feat, hid), fl),
        ),
        in_specs=[pl.BlockSpec(memory_space=pltpu.HBM)] * 3
        + [pl.BlockSpec(memory_space=pltpu.SMEM), pl.BlockSpec(memory_space=pltpu.HBM)],
        out_specs=[pl.BlockSpec(memory_space=pltpu.VMEM)] * 3,
        scratch_shapes=[
            pltpu.VMEM(weight.shape, bf),
            pltpu.VMEM(tile_vals.shape[2:], bf),
            pltpu.VMEM(cotangent.shape, bf),
            pltpu.VMEM((sections, rows, rows), bf),
            pltpu.VMEM((sections, rows, feat), bf),
            pltpu.VMEM((rows, feat), fl),
            pltpu.VMEM((reps, share, feat), bf),
            pltpu.VMEM((reps, share, feat), bf),
            pltpu.VMEM((reps, share, feat), bf),
            pltpu.VMEM((4, feat, rows), fl),
            pltpu.VMEM((sections, 2, feat, rows // 2), bf),
            pltpu.VMEM((sections, 2, feat, rows // 2), bf),
            pltpu.VMEM((reps, share, feat), bf),
            pltpu.VMEM((reps, share, feat), bf),
            pltpu.VMEM((reps, wshare, hid), fl),
            pltpu.VMEM((reps, wshare, hid), fl),
            pltpu.VMEM((wshare, hid), fl),
            pltpu.VMEM((span, wshare, hid), fl),
            pltpu.VMEM((wshare, hid), fl),
            pltpu.VMEM((turns, wshare, hid), fl),
            pltpu.VMEM((reps, wshare, hid), fl),
        ]
        + [pltpu.SemaphoreType.DMA(shape) for shape in sems],
        compiler_params=pltpu.CompilerParams(
            collective_id=0, has_side_effects=True, vmem_limit_bytes=63 << 20
        ),
    )(features, weight, tile_vals[0, 0], codes, cotangent)
    return (act, feat_grad, weight_grad)


def solution(mesh):
    placed = (
        P("blk", None),
        P(),
        P("blk", "rep", None, None, None, None),
        P("blk", "rep", None, None),
        P("blk", "rep", None),
        P(("blk", "rep"), None),
    )
    return jax.shard_map(
        local,
        mesh=mesh,
        in_specs=placed,
        out_specs=(P(("blk", "rep"), None), P(("blk", "rep"), None), P()),
        check_vma=False,
    )
```

```python
import functools
import math

import jax
import jax.numpy as jnp
from jax import lax
from jax.experimental import pallas as pl
from jax.experimental.pallas import tpu as pltpu
from jax.sharding import PartitionSpec as P

MESH = pl.DeviceIdType.MESH


def slot_codes(positions, counts, cells):
    slots = jnp.arange(positions.shape[1], dtype=jnp.int32)[None, None, :]
    hits = positions[:, None, :] == jnp.arange(cells, dtype=jnp.int32)[None, :, None]
    hits = hits & (slots < counts[:, None, None])
    return jnp.sum(jnp.where(hits, slots + 1, 0), axis=-1, dtype=jnp.int32)


def gelu_and_slope(value):
    scale = math.sqrt(2.0 / math.pi)
    square = value * value
    bend = jnp.tanh(scale * (value + 0.044715 * (square * value)))
    half = 0.5 * (1.0 + bend)
    slope = half + 0.5 * value * (1.0 - bend * bend) * (
        scale * (1.0 + 3.0 * 0.044715 * square)
    )
    return value * half, slope


def dot(left, right, contract=(1, 0)):
    return lax.dot_general(
        left,
        right,
        (((contract[0],), (contract[1],)), ((), ())),
        preferred_element_type=jnp.float32,
    )


def layer_kernel(
    blks,
    reps,
    features_ref,
    weight_hbm,
    tiles_hbm,
    code_ref,
    cot_hbm,
    act_ref,
    feat_ref,
    wgrad_ref,
    weight_ref,
    tiles_ref,
    cot_ref,
    adj_ref,
    xs,
    total,
    ysend,
    yrecv,
    urows,
    kept,
    psend,
    precv,
    hsend,
    hrecv,
    wsend,
    wrecv,
    q_out,
    q_in,
    z_out,
    z_in,
    wall,
    load_sems,
    x_ss,
    x_rs,
    y_ss,
    y_rs,
    u_ss,
    u_rs,
    p_ss,
    p_rs,
    h_ss,
    h_rs,
    w_ss,
    w_rs,
    q_ss,
    q_rs,
    z_ss,
    z_rs,
    g_ss,
    g_rs,
):
    b = lax.axis_index("blk")
    r = lax.axis_index("rep")
    sections = blks // reps
    share = cot_ref.shape[0]
    rows = features_ref.shape[0]

    span = 2 * reps
    turns = sections // 2
    z = lax.div(b, span)
    q = lax.rem(b, span)

    def ahead(s):
        return (z * span + lax.rem(q + r + reps * s, span), r)

    def behind(s):
        return (z * span + lax.rem(q - r - reps * s + 2 * span, span), r)

    up = (lax.rem(z + 1, turns) * span + q, r)
    down = (lax.rem(z + turns - 1, turns) * span + q, r)

    def section_of(g, s):
        wrapped = (q - r - reps * s < 0).astype(jnp.int32)
        return lax.rem(2 * (g - wrapped) + s + sections, sections)

    def rep_peer(i):
        return (b, lax.rem(r + i, reps))

    def q_peer(i):
        return (z * span + lax.rem(q + i, span), r)

    def z_peer(i):
        return (lax.rem(z + i, turns) * span + q, r)

    def remote(src, dst, ss, rs, device):
        return pltpu.make_async_remote_copy(
            src_ref=src,
            dst_ref=dst,
            send_sem=ss,
            recv_sem=rs,
            device_id=device,
            device_id_type=MESH,
        )

    loads = [
        pltpu.make_async_copy(source, target, load_sems.at[i])
        for i, (source, target) in enumerate(
            ((tiles_hbm, tiles_ref), (weight_hbm, weight_ref), (cot_hbm, cot_ref))
        )
    ]
    for load in loads:
        load.start()

    barrier = pltpu.get_barrier_semaphore()

    def greet(device):
        pl.semaphore_signal(barrier, inc=1, device_id=device, device_id_type=MESH)

    @pl.when(r != 0)
    def _():
        greet(ahead(0))
        greet(behind(0))

    greet(ahead(1))
    greet(behind(1))
    greet(up)
    greet(down)
    for i in range(1, turns):
        greet(z_peer(i))
    for i in range(1, span):
        greet(q_peer(i))
    for i in range(1, reps):
        greet(rep_peer(i))
    greeted = 4 + (turns - 1) + (span - 1) + (reps - 1)
    pl.semaphore_wait(barrier, jnp.where(r == 0, greeted, greeted + 2))

    part_rows = rows // 2

    def x_copy(g, s, c):
        at = 2 * g + s
        piece = pl.ds(c * part_rows, part_rows)
        if g == 0:
            source, device = features_ref, ahead(s)
        elif g == 1:
            source, device = xs.at[s], up
        elif g == 3:
            source, device = xs.at[s], down
        else:
            source, device = xs.at[2 if s == 0 else 7], (up if s == 0 else down)
        return remote(
            source.at[piece], xs.at[at, piece], x_ss.at[at, c], x_rs.at[at, c], device
        )

    def own_x(c):
        piece = pl.ds(c * part_rows, part_rows)
        return pltpu.make_async_copy(features_ref.at[piece], xs.at[0, piece], x_rs.at[0, c])

    for c in range(2):

        @pl.when(r != 0)
        def _():
            x_copy(0, 0, c).start()

        @pl.when(r == 0)
        def _():
            own_x(c).start()

        x_copy(0, 1, c).start()

    tile = tiles_ref.shape[-1]
    blocks = rows // tile

    def place(j, carry):
        for n in range(blocks):
            for m in range(blocks):
                code = code_ref[j, n * blocks + m]
                picked = tiles_ref[j, jnp.maximum(code - 1, 0)]
                adj_ref[j, n * tile : (n + 1) * tile, m * tile : (m + 1) * tile] = jnp.where(
                    code > 0, picked, jnp.zeros_like(picked)
                )
        return carry

    loads[0].wait()
    lax.fori_loop(0, sections, place, 0)
    loads[1].wait()
    loads[2].wait()

    def term(g, s):
        return dot(adj_ref[section_of(g, s)], xs[2 * g + s])

    for c in range(2):

        @pl.when(r != 0)
        def _():
            x_copy(0, 0, c).wait_recv()

        @pl.when(r == 0)
        def _():
            own_x(c).wait()

        x_copy(1, 0, c).start()
        x_copy(3, 0, c).start()
        x_copy(0, 1, c).wait_recv()
        x_copy(3, 1, c).start()
        x_copy(1, 1, c).start()

    total[...] = term(0, 0) + term(0, 1)
    for c in range(2):
        x_copy(1, 0, c).wait_recv()
        x_copy(2, 0, c).start()
        x_copy(3, 1, c).wait_recv()
        x_copy(2, 1, c).start()
    total[...] += term(1, 0) + term(3, 1)
    for g, s in ((3, 0), (1, 1), (2, 0), (2, 1)):
        x_copy(g, s, 0).wait_recv()
        x_copy(g, s, 1).wait_recv()
        total[...] += term(g, s)

    ysend[...] = total[...].astype(jnp.bfloat16).reshape(ysend.shape)

    def to_peers(copy, count):
        for i in range(1, count):
            copy(i).start()

    def take(copy, count):
        for i in range(1, count):
            copy(i).wait_recv()

    def y_copy(i):
        peer = rep_peer(i)
        return remote(ysend.at[peer[1]], yrecv.at[i], y_ss.at[i], y_rs.at[i], peer)

    to_peers(y_copy, reps)
    mixed = ysend[r].astype(jnp.float32)
    for i in range(1, reps):
        y_copy(i).wait_recv()
        mixed = mixed + yrecv[i].astype(jnp.float32)

    weight = weight_ref[...]
    high = mixed.astype(jnp.bfloat16)
    low = (mixed - high.astype(jnp.float32)).astype(jnp.bfloat16)
    act, slope = gelu_and_slope(dot(high, weight) + dot(low, weight))
    act_ref[...] = act.astype(jnp.bfloat16)
    pre_grad = (cot_ref[...].astype(jnp.float32) * slope).astype(jnp.bfloat16)
    urows[r] = dot(pre_grad, weight, (1, 1)).astype(jnp.bfloat16)

    def u_copy(i):
        return remote(urows.at[r], urows.at[r], u_ss.at[i], u_rs.at[i], rep_peer(i))

    def u_arrival(i):
        source = lax.rem(r - i + reps, reps)
        return remote(urows.at[source], urows.at[source], u_ss.at[i], u_rs.at[i], rep_peer(i))

    to_peers(u_copy, reps)
    wsend[...] = dot(high, pre_grad, (0, 0)).reshape(wsend.shape)

    def w_copy(i):
        peer = rep_peer(i)
        return remote(wsend.at[peer[1]], wrecv.at[i], w_ss.at[i], w_rs.at[i], peer)

    to_peers(w_copy, reps)
    take(u_arrival, reps)
    flipped = urows[...].reshape(rows, urows.shape[2]).T

    def p_copy(at, c):
        device = (down, up, down, down, up, up, behind(0), behind(1))[at]
        return remote(psend.at[at, c], precv.at[at, c], p_ss.at[at, c], p_rs.at[at, c], device)

    def own_p(c):
        return pltpu.make_async_copy(psend.at[6, c], precv.at[6, c], p_rs.at[6, c])

    def back(g, s):
        return dot(flipped, adj_ref[section_of(g, s)])

    def half(value, c):
        return value[:, c * part_rows : (c + 1) * part_rows]

    def arrived(at, c):
        p_copy(at, c).wait_recv()
        return precv[at, c].astype(jnp.float32)

    for pair in (((0, 2, 0), (1, 2, 1)), ((3, 1, 1), (4, 3, 0))):
        for at, g, s in pair:
            value = back(g, s).astype(jnp.bfloat16)
            psend[at, 0] = half(value, 0)
            psend[at, 1] = half(value, 1)
            p_copy(at, 0).start()
            p_copy(at, 1).start()
    for at, g, s in ((0, 0, 0), (1, 0, 1), (2, 1, 0), (3, 3, 1)):
        kept[at] = back(g, s)

    part = wsend[r]
    for i in range(1, reps):
        w_copy(i).wait_recv()
        part = part + wrecv[i]
    q_out[...] = part

    def q_copy(i):
        return remote(q_out, q_in.at[i], q_ss.at[i], q_rs.at[i], q_peer(i))

    to_peers(q_copy, span)

    for c in range(2):
        for near, at in ((0, 2), (1, 5)):
            mine = half(kept[2 + near], c)
            psend[at, c] = (mine + arrived(near, c)).astype(jnp.bfloat16)
            p_copy(at, c).start()

    for i in range(1, span):
        q_copy(i).wait_recv()
        part = part + q_in[i]
    z_out[...] = part

    def z_copy(i):
        return remote(z_out, z_in.at[i], z_ss.at[i], z_rs.at[i], z_peer(i))

    to_peers(z_copy, turns)

    for c in range(2):
        psend[7, c] = (half(kept[1], c) + arrived(3, c) + arrived(5, c)).astype(jnp.bfloat16)
        p_copy(7, c).start()
        psend[6, c] = (half(kept[0], c) + arrived(2, c) + arrived(4, c)).astype(jnp.bfloat16)

        @pl.when(r != 0)
        def _():
            p_copy(6, c).start()

        @pl.when(r == 0)
        def _():
            own_p(c).start()

    for i in range(1, turns):
        z_copy(i).wait_recv()
        part = part + z_in[i]
    wall[r] = part

    def g_copy(i):
        return remote(wall.at[r], wall.at[r], g_ss.at[i], g_rs.at[i], rep_peer(i))

    def g_arrival(i):
        source = lax.rem(r - i + reps, reps)
        return remote(wall.at[source], wall.at[source], g_ss.at[i], g_rs.at[i], rep_peer(i))

    to_peers(g_copy, reps)

    def owned(c):
        @pl.when(r != 0)
        def _():
            p_copy(6, c).wait_recv()

        @pl.when(r == 0)
        def _():
            own_p(c).wait()

        return precv[6, c].astype(jnp.float32) + arrived(7, c)

    for c in range(2):
        kept[0, :, c * part_rows : (c + 1) * part_rows] = owned(c)
    summed = kept[0]
    hsend[...] = summed.T.astype(jnp.bfloat16).reshape(hsend.shape)

    def h_copy(i):
        peer = rep_peer(i)
        return remote(hsend.at[peer[1]], hrecv.at[i], h_ss.at[i], h_rs.at[i], peer)

    to_peers(h_copy, reps)
    rows_grad = hsend[r].astype(jnp.float32)
    for i in range(1, reps):
        h_copy(i).wait_recv()
        rows_grad = rows_grad + hrecv[i].astype(jnp.float32)
    feat_ref[...] = rows_grad.astype(jnp.bfloat16)
    take(g_arrival, reps)
    wgrad_ref[...] = wall[...].reshape(wgrad_ref.shape)

    for c in range(2):

        @pl.when(r != 0)
        def _():
            x_copy(0, 0, c).wait_send()
            p_copy(6, c).wait_send()

        x_copy(0, 1, c).wait_send()
        for g in range(1, 4):
            x_copy(g, 0, c).wait_send()
            x_copy(g, 1, c).wait_send()
        for at in (0, 1, 2, 3, 4, 5, 7):
            p_copy(at, c).wait_send()
    for i in range(1, turns):
        z_copy(i).wait_send()
    for i in range(1, span):
        q_copy(i).wait_send()
    for i in range(1, reps):
        y_copy(i).wait_send()
        u_copy(i).wait_send()
        w_copy(i).wait_send()
        h_copy(i).wait_send()
        g_copy(i).wait_send()


def local(features, weight, tile_vals, tile_pos, tile_count, cotangent):
    reps = lax.axis_size("rep")
    blks = lax.axis_size("blk")
    sections = blks // reps
    rows, feat = features.shape
    hid = weight.shape[1]
    share = rows // reps
    wshare = feat // reps
    blocks = rows // tile_vals.shape[-1]
    codes = slot_codes(tile_pos[0, 0], tile_count[0, 0], blocks * blocks)
    bf, fl = jnp.bfloat16, jnp.float32
    span, turns = 2 * reps, sections // 2
    halves = (sections, 2)
    sems = [(3,)] + [halves] * 2 + [(reps,)] * 4 + [halves] * 2 + [(reps,)] * 4
    sems += [(span,)] * 2 + [(turns,)] * 2 + [(reps,)] * 2
    act, feat_grad, weight_grad = pl.pallas_call(
        functools.partial(layer_kernel, blks, reps),
        out_shape=(
            jax.ShapeDtypeStruct((share, hid), bf),
            jax.ShapeDtypeStruct((share, feat), bf),
            jax.ShapeDtypeStruct((feat, hid), fl),
        ),
        in_specs=[pl.BlockSpec(memory_space=pltpu.HBM)] * 3
        + [pl.BlockSpec(memory_space=pltpu.SMEM), pl.BlockSpec(memory_space=pltpu.HBM)],
        out_specs=[pl.BlockSpec(memory_space=pltpu.VMEM)] * 3,
        scratch_shapes=[
            pltpu.VMEM(weight.shape, bf),
            pltpu.VMEM(tile_vals.shape[2:], bf),
            pltpu.VMEM(cotangent.shape, bf),
            pltpu.VMEM((sections, rows, rows), bf),
            pltpu.VMEM((sections, rows, feat), bf),
            pltpu.VMEM((rows, feat), fl),
            pltpu.VMEM((reps, share, feat), bf),
            pltpu.VMEM((reps, share, feat), bf),
            pltpu.VMEM((reps, share, feat), bf),
            pltpu.VMEM((4, feat, rows), fl),
            pltpu.VMEM((sections, 2, feat, rows // 2), bf),
            pltpu.VMEM((sections, 2, feat, rows // 2), bf),
            pltpu.VMEM((reps, share, feat), bf),
            pltpu.VMEM((reps, share, feat), bf),
            pltpu.VMEM((reps, wshare, hid), fl),
            pltpu.VMEM((reps, wshare, hid), fl),
            pltpu.VMEM((wshare, hid), fl),
            pltpu.VMEM((span, wshare, hid), fl),
            pltpu.VMEM((wshare, hid), fl),
            pltpu.VMEM((turns, wshare, hid), fl),
            pltpu.VMEM((reps, wshare, hid), fl),
        ]
        + [pltpu.SemaphoreType.DMA(shape) for shape in sems],
        compiler_params=pltpu.CompilerParams(
            collective_id=0, has_side_effects=True, vmem_limit_bytes=53 << 20
        ),
    )(features, weight, tile_vals[0, 0], codes, cotangent)
    return (act, feat_grad, weight_grad)


def solution(mesh):
    placed = (
        P("blk", None),
        P(),
        P("blk", "rep", None, None, None, None),
        P("blk", "rep", None, None),
        P("blk", "rep", None),
        P(("blk", "rep"), None),
    )
    return jax.shard_map(
        local,
        mesh=mesh,
        in_specs=placed,
        out_specs=(P(("blk", "rep"), None), P(("blk", "rep"), None), P()),
        check_vma=False,
    )
```
